32 devices in a mesh: gx: 2 (over y), gy: 4 (over x, core), gz: 4 (over z).
Axes of the slice: x: 2, y: 2, z: 4, core: 2. Of those that a mesh axis runs over, the one named last changes fastest.
Arguments:
- phase_stack: float32 [512, 65536], P(None, ('gx', 'gy', 'gz')), may hold values from -40 to 40
- start_basis: float32 [512, 64], replicated, may hold values from -6 to 6
Outputs:
- corrected: float32 [512, 65536], P(None, ('gx', 'gy', 'gz'))
The draws below stay inside these ranges and needn't reach their ends.
All inputs are finite; a program needn't handle non-finite values.
Results may differ from the reference program's by a relative error of at most 0.0003.
Values sent between devices are 32-bit elements; how exact they have to be, the bound alone decides.
A program may use at most 64 MiB of HBM per device.

```python
import math
import jax
import jax.numpy as jnp
from jax import lax

M = 512
K = 64
ITERS = 3
NPIX = 65536


def draw_phase_stack(key, part):
    base = jax.random.fold_in(key, 11)
    key_mix = jax.random.fold_in(base, 0)
    key_amp = jax.random.fold_in(base, 1)
    key_src = jax.random.fold_in(base, 2)
    key_clutter = jax.random.fold_in(base, 4)
    mixing = jax.random.normal(key_mix, (M, K), jnp.float32) / math.sqrt(M)
    amplitude = jnp.exp(jax.random.uniform(key_amp, (K,), jnp.float32, 0.0, math.log(4.2)))
    sources = jax.random.normal(key_src, (K, NPIX), jnp.float32)
    position = jnp.arange(NPIX, dtype=jnp.float32) / NPIX
    clutter_scale = 1.0 + 2.0 * position
    clutter = jax.random.normal(key_clutter, (M, NPIX), jnp.float32)
    signal = jnp.dot(mixing * amplitude[None, :], sources, precision=lax.Precision.HIGHEST)
    return jnp.clip(signal + clutter * clutter_scale[None, :], -40.0, 40.0)


def centred(key, shape, spread, most, kind=jnp.bfloat16):
    array = spread * jax.random.normal(key, shape, jnp.float32)
    return jnp.clip(array, min=-most, max=most).astype(kind)


def setup_inputs(seed: int = 0) -> dict:
    splits = jax.random.split(jax.random.key(seed), 3)
    return {
        "phase_stack": draw_phase_stack(jax.random.fold_in(splits[2], 71), 0),
        "start_basis": centred(splits[1], (M, K), 1.0, 6.0, jnp.float32),
    }


HIGHEST = lax.Precision.HIGHEST
EPSILON = 1e-06

def orthonormal(columns):
    inner_gram = jnp.dot(columns.T, columns, precision=HIGHEST)
    cholesky_factor = jnp.linalg.cholesky(inner_gram)
    return jax.scipy.linalg.solve_triangular(cholesky_factor, columns.T, lower=True).T

def reference(phase_stack, start_basis):
    pixel_total = phase_stack.shape[1]
    gram_matrix = jnp.dot(phase_stack, phase_stack.T, precision=HIGHEST) / pixel_total
    subspace = orthonormal(start_basis)
    for sweep in range(ITERS):
        subspace = orthonormal(jnp.dot(gram_matrix, subspace, precision=HIGHEST))
    loadings = jnp.dot(subspace.T, phase_stack, precision=HIGHEST)
    residual = phase_stack - jnp.dot(subspace, loadings, precision=HIGHEST)
    row_power = lax.optimization_barrier(jnp.sum(residual * residual, axis=1)) / pixel_total
    return residual * lax.rsqrt(row_power + EPSILON)[:, None]
```

```python
import functools
import itertools

import jax
import jax.numpy as jnp
from jax import lax
from jax.experimental import pallas as pl
from jax.experimental.pallas import tpu as pltpu
from jax.sharding import PartitionSpec as P

ITERS = 3
EPSILON = 1e-06
HIGHEST = lax.Precision.HIGHEST
MESH = pl.DeviceIdType.MESH
AXES = ("gx", "gy", "gz")
F32 = jnp.float32
BF16 = jnp.bfloat16
LANES = 128
STRIP = 1024
PIECES = 5
STEPS = (4, 4)


def split(value):
    high = value.astype(BF16)
    return high, (value - high.astype(F32)).astype(BF16)


def dot_nt(a, b, **kw):
    return lax.dot_general(a, b, (((1,), (1,)), ((), ())), preferred_element_type=F32, **kw)


def dot_tn(a, b, **kw):
    return lax.dot_general(a, b, (((0,), (0,)), ((), ())), preferred_element_type=F32, **kw)


def dot_nn(a, b, **kw):
    return lax.dot_general(a, b, (((1,), (0,)), ((), ())), preferred_element_type=F32, **kw)


def orthonormal_steps(rows):
    k = rows.shape[0]
    inner = dot_nt(rows, rows, precision=HIGHEST)
    eye = (
        lax.broadcasted_iota(jnp.int32, (k, k), 0) == lax.broadcasted_iota(jnp.int32, (k, k), 1)
    ).astype(F32)
    work = jnp.concatenate([eye, inner], axis=1)
    groups = [work[g : g + 8] for g in range(0, k, 8)]
    wide = (8, 2 * k)
    sub = lax.broadcasted_iota(jnp.int32, wide, 0)

    def across(value, lane):
        return jnp.broadcast_to(value[:, lane : lane + 1], wide)

    def down(value, row):
        return jnp.broadcast_to(value[row : row + 1], wide)

    def stack(entries):
        out = jnp.zeros(wide, F32)
        for row, entry in entries:
            out = jnp.where(sub == row, entry, out)
        return out

    def tree(terms):
        while len(terms) > 1:
            terms = [sum(terms[t + 1 : t + 2], terms[t]) for t in range(0, len(terms), 2)]
        return terms[0]

    finished = []
    for home in range(len(groups)):
        base = k + 8 * home
        panel = groups[home]
        columns = [across(panel, base + j) for j in range(8)]
        below = [[across(groups[g], base + j) for j in range(8)] for g in range(home + 1, k // 8)]
        e = [[down(columns[j], i) for j in range(i + 1)] for i in range(8)]
        low = [[None] * 8 for _ in range(8)]
        roots = []
        for j in range(8):
            inv = 1.0 / e[j][j]
            roots.append(lax.rsqrt(e[j][j]))
            for i in range(j + 1, 8):
                low[i][j] = e[i][j] * inv
            for i in range(j + 1, 8):
                for c in range(j + 1, i + 1):
                    e[i][c] = e[i][c] - low[i][j] * e[c][j]
        w = [[None] * 8 for _ in range(8)]
        for i in range(8):
            for j in range(i):
                terms = [low[i][j]] + [low[i][c] * w[c][j] for c in range(j + 1, i)]
                w[i][j] = -tree(terms)
        for i in range(8):
            for j in range(i):
                w[i][j] = w[i][j] * roots[i]
            w[i][i] = roots[i]
        panel = tree(
            [stack([(i, w[i][j]) for i in range(j, 8)]) * down(panel, j) for j in range(8)]
        )
        finished.append(panel)
        if below:
            back = tree(
                [stack([(j, w[i][j]) for j in range(i + 1)]) * down(panel, i) for i in range(8)]
            )
            back = [down(back, j) for j in range(8)]
            for g, cols in enumerate(below):
                at = home + 1 + g
                groups[at] = groups[at] - tree([c * r for c, r in zip(cols, back)])
        yield None
    inverse = jnp.concatenate(finished, axis=0)[:, :k]
    yield dot_nn(inverse, rows, precision=HIGHEST)


def orthonormal_rows(rows):
    *_, result = orthonormal_steps(rows)
    return result


def pieces(m, n):
    nb = m // LANES
    blocks = [(i, j) for i in range(nb) for j in range(i, nb)]
    rows = len(blocks) * LANES // n
    out = []
    for b, (i, j) in enumerate(blocks):
        at, end = b * LANES, (b + 1) * LANES
        while at < end:
            chunk, low = divmod(at, rows)
            take = min(end - at, rows - low)
            out.append((chunk, low, i, j, at - b * LANES, take))
            at += take
    return rows, out


def pack_shape(shape):
    return 2, shape[0] * (shape[1] // 2), PIECES


def slot(chunk, dims):
    out = []
    for size in reversed(dims):
        chunk, at = divmod(chunk, size)
        out.append(at)
    return tuple(reversed(out))


def kernel(
    shape, x_hbm, basis_hbm, res_ref, scale_ref,
    x, basis, xh, xl, half, cross, packed, pair_in, middle, plane_in, part, column_in, total,
    gh, gl, vt, own, sums,
    x_sem, basis_sem, send_sem, pair_sem, plane_sem, column_sem, out_sem, back_sem, sums_sem,
):
    n = shape[0] * shape[1] * shape[2]
    m, width = x.shape
    me = (lax.axis_index("gx") * shape[1] + lax.axis_index("gy")) * shape[2] + lax.axis_index("gz")
    dims = pack_shape(shape)
    planes, columns = dims[1], shape[2]
    _, plan = pieces(m, dims[0] * dims[1] * dims[2])
    gx, gy, gz = (lax.axis_index(axis) for axis in AXES)
    side, plane = lax.rem(gy, 2), gx * (shape[1] // 2) + gy // 2
    half_gy = shape[1] // 2
    strips = width // STRIP

    def strip(s):
        return pl.ds(pl.multiple_of(s * STRIP, STRIP), STRIP)

    def fetch(s):
        return pltpu.make_async_copy(x_hbm.at[:, strip(s)], x.at[:, strip(s)], x_sem.at[s])

    for s in range(strips):
        fetch(s).start()

    load_basis = pltpu.make_async_copy(basis_hbm, basis, basis_sem)
    load_basis.start()

    barrier = pltpu.get_barrier_semaphore()

    others = sorted(
        itertools.product(*map(range, shape)),
        key=lambda step: -sum(min(d, size - d) for d, size in zip(step, shape)),
    )[:-1]
    here = (gx, gy, gz)
    others = [
        tuple(lax.rem(at + d, size) if d else at for at, d, size in zip(here, step, shape))
        for step in others
    ]
    for peer in others:
        pl.semaphore_signal(barrier, inc=1, device_id=peer, device_id_type=MESH)

    half[...] = jnp.zeros_like(half)
    cross[...] = jnp.zeros_like(cross)

    @pl.loop(0, strips)
    def _(s):
        fetch(s).wait()
        high, low = split(x[:, strip(s)])
        xh[:, strip(s)] = high
        xl[:, strip(s)] = low
        cross[...] += dot_nt(high, low)
        half[: m // 2] += dot_nt(high[: m // 2], high)
        half[m // 2 :, m // 2 :] += dot_nt(high[m // 2 :], high[m // 2 :])

    half[...] += cross[...] + cross[...].T
    for chunk, low, i, j, start, take in plan:
        packed[slot(chunk, dims) + (slice(low, low + take),)] = half[
            i * LANES + start : i * LANES + start + take, j * LANES : (j + 1) * LANES
        ]

    pl.semaphore_wait(barrier, n - 1)

    def send(stage, source, target, arrival, peer):
        pltpu.make_async_remote_copy(
            src_ref=source,
            dst_ref=target,
            send_sem=send_sem.at[stage],
            recv_sem=arrival,
            device_id=peer,
            device_id_type=MESH,
        ).start()

    def landed(target, arrival):
        pltpu.make_async_copy(target, target, arrival).wait()

    partner = (gx, gy + 1 - 2 * side, gz)

    def in_plane(index):
        return (index // half_gy, 2 * (index % half_gy) + side, gz)

    def other_plane(d):
        return lax.rem(plane + d, planes)

    def other_column(d):
        return lax.rem(gz + d, columns)

    away_first = [*range(1, planes), 0]
    basis_steps = []

    def work(steps=1):
        for _ in range(steps):
            for step in basis_steps:
                step = next(step, None)
                if step is not None:
                    vt[...] = step

    for p in range(PIECES):
        for d in away_first:
            q = other_plane(d)
            send(0, packed.at[1 - side, q, p], pair_in.at[q, p], pair_sem.at[q, p], partner)
    load_basis.wait()
    for p in range(PIECES):
        for d in away_first:
            q = other_plane(d)
            landed(pair_in.at[q, p], pair_sem.at[q, p])
            middle[q, p] = packed[side, q, p] + pair_in[q, p]
            if d:
                send(1, middle.at[q, p], plane_in.at[plane, p], plane_sem.at[plane, p], in_plane(q))
    basis_steps.append(orthonormal_steps(basis[...]))
    work(STEPS[0])
    for p in range(PIECES):
        value = middle[plane, p]
        for d in range(1, planes):
            q = other_plane(d)
            landed(plane_in.at[q, p], plane_sem.at[q, p])
            value = value + plane_in[q, p]
        part[p] = value
        for d in range(1, columns):
            c = other_column(d)
            send(2, part.at[p], column_in.at[gz, p], column_sem.at[gz, p], (gx, gy, c))
        column_in[gz, p] = value
    work(STEPS[1])
    for p in range(PIECES):
        for d in range(1, columns):
            c = other_column(d)
            landed(column_in.at[c, p], column_sem.at[c, p])
        value = column_in[0, p]
        for c in range(1, columns):
            value = value + column_in[c, p]
        total[side, plane, p] = value * (1.0 / (n * width))
        ready = total.at[side, plane, p]
        for d in range(1, planes):
            send(3, ready, ready, out_sem.at[plane, p], in_plane(other_plane(d)))
        send(4, ready, ready, back_sem, partner)
    work(99)
    for p in range(PIECES):
        for d in range(1, planes):
            q = other_plane(d)
            ready = total.at[side, q, p]
            landed(ready, out_sem.at[q, p])
            send(4, ready, ready, back_sem, partner)
    landed(total.at[1 - side], back_sem)

    for chunk, low, i, j, start, take in plan:
        half[
            i * LANES + start : i * LANES + start + take, j * LANES : (j + 1) * LANES
        ] = total[slot(chunk, dims) + (slice(low, low + take),)]
    for i in range(m // LANES):
        for j in range(i):
            rows, cols = pl.ds(i * LANES, LANES), pl.ds(j * LANES, LANES)
            half[rows, cols] = half[cols, rows].T
    high, low = split(half[...])
    gh[...] = high
    gl[...] = low

    def advance(_, carry):
        vh, vl = split(vt[...])
        both = dot_nn(jnp.concatenate([vh, vl], axis=0), gh[...])
        k = vh.shape[0]
        fresh = both[:k] + both[k:] + dot_nn(vh, gl[...])
        vt[...] = orthonormal_rows(fresh)
        return carry

    lax.fori_loop(0, ITERS, advance, 0, unroll=True)

    vh, vl = split(vt[...])
    k = vh.shape[0]
    tall = jnp.concatenate([vh, vl], axis=0)
    left = jnp.concatenate([vh, vh, vl], axis=0).T

    def strip_power(s, power):
        both = dot_nn(tall, xh[:, strip(s)])
        loadings = both[:k] + both[k:] + dot_nn(vh, xl[:, strip(s)])
        lh, ll = split(loadings)
        residual = x[:, strip(s)] - dot_nn(left, jnp.concatenate([lh, ll, lh], axis=0))
        res_ref[:, strip(s)] = residual
        square = residual * residual
        for c in range(0, STRIP, LANES):
            power = power + square[:, c : c + LANES]
        return power

    power = lax.fori_loop(0, strips, strip_power, jnp.zeros((m, LANES), F32), unroll=True)
    own[...] = jnp.sum(power.T, axis=0, keepdims=True)
    for peer in others:
        send(5, own, sums.at[me], sums_sem, peer)

    sums[me] = own[...]
    landed(sums.at[pl.ds(0, n - 1)], sums_sem)
    row_power = jnp.sum(sums[...], axis=0) * (1.0 / (n * width))
    scale = lax.rsqrt(row_power + EPSILON)
    scale_ref[...] = jnp.broadcast_to(scale, (LANES, m)).T
    for stage, whole in enumerate([
        total.at[0],
        total.at[0, pl.ds(0, planes - 1)],
        column_in.at[pl.ds(0, columns - 1)],
        total.at[0, pl.ds(0, planes - 1)],
        total.at[0],
        sums.at[pl.ds(0, n - 1)],
    ]):
        landed(whole, send_sem.at[stage])


def on_device(shape, phase_stack, start_basis):
    m, width = phase_stack.shape
    k = start_basis.shape[1]
    n = shape[0] * shape[1] * shape[2]
    assert shape[1] % 2 == 0
    sides, planes, _ = pack_shape(shape)
    columns = shape[2]
    chunk_rows, _ = pieces(m, sides * planes * PIECES)
    chunk = (PIECES, chunk_rows, LANES)
    vmem = pl.BlockSpec(memory_space=pltpu.VMEM)
    residual, scale = pl.pallas_call(
        functools.partial(kernel, shape),
        out_shape=(
            jax.ShapeDtypeStruct((m, width), F32),
            jax.ShapeDtypeStruct((m, LANES), F32),
        ),
        in_specs=[pl.BlockSpec(memory_space=pltpu.HBM)] * 2,
        out_specs=(vmem, vmem),
        scratch_shapes=[
            pltpu.VMEM((m, width), F32),
            pltpu.VMEM((k, m), F32),
            pltpu.VMEM((m, width), BF16),
            pltpu.VMEM((m, width), BF16),
            pltpu.VMEM((m, m), F32),
            pltpu.VMEM((m, m), F32),
            pltpu.VMEM((sides, planes, *chunk), F32),
            pltpu.VMEM((planes, *chunk), F32),
            pltpu.VMEM((planes, *chunk), F32),
            pltpu.VMEM((planes, *chunk), F32),
            pltpu.VMEM(chunk, F32),
            pltpu.VMEM((columns, *chunk), F32),
            pltpu.VMEM((sides, planes, *chunk), F32),
            pltpu.VMEM((m, m), BF16),
            pltpu.VMEM((m, m), BF16),
            pltpu.VMEM((k, m), F32),
            pltpu.VMEM((1, m), F32),
            pltpu.VMEM((n, 1, m), F32),
            pltpu.SemaphoreType.DMA((width // STRIP,)),
            pltpu.SemaphoreType.DMA,
            pltpu.SemaphoreType.DMA((6,)),
            pltpu.SemaphoreType.DMA((planes, PIECES)),
            pltpu.SemaphoreType.DMA((planes, PIECES)),
            pltpu.SemaphoreType.DMA((columns, PIECES)),
            pltpu.SemaphoreType.DMA((planes, PIECES)),
            pltpu.SemaphoreType.DMA,
            pltpu.SemaphoreType.DMA,
        ],
        compiler_params=pltpu.CompilerParams(
            collective_id=0, has_side_effects=True, vmem_limit_bytes=40 << 20
        ),
        name="common_mode",
    )(
        pltpu.with_memory_space_constraint(phase_stack, pltpu.HBM),
        pltpu.with_memory_space_constraint(start_basis.T, pltpu.HBM),
    )
    return residual * scale[:, :1]


def solution(mesh):
    shape = tuple(mesh.shape[a] for a in AXES)
    return jax.shard_map(
        functools.partial(on_device, shape),
        mesh=mesh,
        in_specs=(P(None, AXES), P()),
        out_specs=P(None, AXES),
        check_vma=False,
    )
```
